32 devices in a mesh: runs: 2 (over x), space: 16 (over z, y, core).
Axes of the slice: x: 2, y: 2, z: 4, core: 2. Of those that a mesh axis runs over, the one named last changes fastest.
Arguments:
- fields: float32 [128, 512], P(('runs', 'space')), parts along dimension 0, may hold values from -3 to 3
- end_weights: bfloat16 [256, 128, 512], P(None, ('runs', 'space')), parts along dimension 1, may hold values from 0.5 to 1.5
- directions: float32 [3, 256], replicated, may hold values from -1 to 1
- analysis: bfloat16 [256, 256], replicated, may hold values from -0.375 to 0.375
- synthesis: bfloat16 [256, 256], replicated, may hold values from -0.375 to 0.375
- decay_rates: float32 [256], replicated, may hold values from 0.1 to 1
Outputs:
- density: float32 [128, 512], P(('runs', 'space')), parts along dimension 0
The draws below stay inside these ranges and needn't reach their ends.
There are 2 independent parts, one for each index of `runs`. The reference program is written for one: setup_inputs(seed, part) draws one part's arguments, and reference() takes and returns one part's arrays. A program takes and returns all parts, laid end to end along the dimension named above; an argument that names none is the same for every part. Nothing has to cross between parts.
All inputs are finite; a program needn't handle non-finite values.
Results may differ from the reference program's by a relative error of at most 0.003.
Values may be sent and summed in bfloat16 or wider, within the bound.
A program may use at most 64 MiB of HBM per device.

```python
import math
import jax
import jax.numpy as jnp

ORIENT = 256
HARM = 256
SX = 4
NY = 32
NZ = 16
STEPS = 4
NX = 32


def steps_of(key, dims, cuts, low, top_value):
    gain = 1.0
    for axis_at, parts in cuts:
        draws = jax.random.uniform(jax.random.fold_in(jax.random.fold_in(key, 6), axis_at), (parts,), jnp.float32, low / len(cuts), top_value / len(cuts))
        gain = gain * jnp.repeat(jnp.exp(draws), dims[axis_at] // parts).reshape((-1,) + (1,) * (len(dims) - 1 - axis_at))
    return gain


def centred(stream_key, extent, spread, most, shards=(), kind=jnp.bfloat16):
    result = jax.random.normal(stream_key, extent, jnp.float32) * spread
    if len(shards) > 0:
        result = steps_of(stream_key, extent, shards, -0.22, 0.18) * result
    return jnp.clip(result, min=-most, max=most).astype(kind)


def setup_inputs(seed: int = 0, part: int = 0) -> dict:
    seeds = jax.random.split(jax.random.key(seed), 7)
    own_keys = jax.random.split(jax.random.fold_in(seeds[6], part), 7)
    return {
        "fields": centred(own_keys[0], (2 * NX, NY * NZ), 0.5, 3.0, ((0, 16),), jnp.float32),
        "end_weights": jnp.clip(0.5 + 1.0 * jax.random.uniform(own_keys[1], (ORIENT, 2 * NX, NY * NZ), jnp.float32) ** steps_of(own_keys[1], (ORIENT, 2 * NX, NY * NZ), ((1, 16),), -0.2, 0.2), 0.5, 1.5).astype(jnp.bfloat16),
        "directions": jnp.clip(jax.random.uniform(seeds[2], (3, ORIENT), jnp.float32, -1.0, 1.0), -1.0, 1.0),
        "analysis": centred(seeds[3], (HARM, ORIENT), ORIENT ** -0.5, 0.375),
        "synthesis": centred(seeds[4], (ORIENT, HARM), HARM ** -0.5, 0.375),
        "decay_rates": jnp.clip(jnp.exp(jax.random.uniform(seeds[5], (HARM,), jnp.float32, math.log(0.1), math.log(1.0))), 0.1, 1.0),
    }


courant = 0.3
slope = 0.6


def advance(current, field, velocity, analysis, synthesis, decay_rates):
    factor = jnp.exp(-0.5 * field)[None]
    shaped = (factor * current.astype(jnp.float32)).astype(jnp.bfloat16)
    center = shaped.astype(jnp.float32)
    drift_sum = jnp.zeros_like(center)
    for component in range(3):
        upwind_pos = jnp.maximum(velocity[component], 0.0)[:, None, None, None]
        upwind_neg = jnp.minimum(velocity[component], 0.0)[:, None, None, None]
        prev_cells = jnp.roll(center, 1, axis=component + 1)
        next_cells = jnp.roll(center, -1, axis=component + 1)
        drift_sum = drift_sum + upwind_pos * (center - prev_cells) + upwind_neg * (next_cells - center)
    moved_cells = (center - courant * drift_sum).astype(jnp.bfloat16)
    flattened = moved_cells.reshape(ORIENT, -1)
    harmonics = (decay_rates[:, None] * jnp.dot(analysis, flattened, preferred_element_type=jnp.float32)).astype(jnp.bfloat16)
    rotated = jnp.mean(flattened.astype(jnp.float32), axis=0, keepdims=True) + jnp.dot(synthesis, harmonics, preferred_element_type=jnp.float32)
    return (factor * rotated.reshape(current.shape)).astype(jnp.bfloat16)


def propagate(start, first_field, second_field, velocity, analysis, synthesis, decay_rates):
    slices = [start]
    current = start
    for step_index in range(STEPS):
        field = first_field if step_index < STEPS // 2 else second_field
        current = advance(current, field, velocity, analysis, synthesis, decay_rates)
        slices.append(current)
    return slices


def pair_sum(own_slices, partner_slices):
    half_steps = STEPS // 2
    running = jnp.zeros(own_slices[0].shape[1:], jnp.float32)
    for position in range(half_steps + 1):
        weight = 0.5 if position in (0, half_steps) else 1.0
        running = running + weight * jnp.mean(own_slices[position].astype(jnp.float32) * partner_slices[STEPS - position].astype(jnp.float32), axis=0)
    return running


def reference(fields, end_weights, directions, analysis, synthesis, decay_rates):
    slabs = NX // SX
    ramp = (slope * jnp.arange(NX).astype(jnp.float32) / NX)[:, None, None]
    split_fields = fields.reshape(slabs, 2, SX, NY, NZ)
    field_a = split_fields[:, 0].reshape(NX, NY, NZ) + ramp
    field_b = split_fields[:, 1].reshape(NX, NY, NZ) + ramp
    split_ends = end_weights.reshape(ORIENT, slabs, 2, SX, NY, NZ)
    start_a = split_ends[:, :, 0].reshape(ORIENT, NX, NY, NZ)
    start_b = split_ends[:, :, 1].reshape(ORIENT, NX, NY, NZ)
    forward_slices = propagate(start_a, field_a, field_b, directions, analysis, synthesis, decay_rates)
    backward_slices = propagate(start_b, field_b, field_a, -directions, analysis, synthesis, decay_rates)
    half_steps = STEPS // 2
    partition = jnp.mean(jnp.mean(forward_slices[half_steps].astype(jnp.float32) * backward_slices[half_steps].astype(jnp.float32), axis=0))
    density_a = pair_sum(forward_slices, backward_slices) / partition
    density_b = pair_sum(backward_slices, forward_slices) / partition
    stacked = jnp.stack([density_a.reshape(slabs, SX, NY * NZ), density_b.reshape(slabs, SX, NY * NZ)], axis=1)
    return stacked.reshape(2 * NX, NY * NZ)
```

```python
import functools

import jax
import jax.numpy as jnp
from jax import lax
from jax.experimental import pallas as pl
from jax.experimental.pallas import tpu as pltpu
from jax.sharding import PartitionSpec as P

NZ = 16
STEPS = 4
HALF = STEPS // 2
YB = 4

courant = 0.3
slope = 0.6

MESH = pl.DeviceIdType.MESH
F32 = jnp.float32
BF16 = jnp.bfloat16


def lane_sum(product):
    ones = jnp.ones((8, product.shape[1]), BF16)
    total = lax.dot_general(ones, product, (((1,), (1,)), ((), ())), preferred_element_type=F32)
    return total[0:1]


def kernel(
    devices, chunk, fields, ends, directions, analysis, synthesis, decay, out,
    state, moved, edges, mixing, column, coef, field_in, half_out,
    x_out, x_in, y_out, y_in, reduced, part_out, part_in, rho_out, rho_in,
    field_sem, ends_sem, x_send, x_recv, y_send, y_recv, part_send, part_recv, rho_sem,
):
    planes, cells = fields.shape
    half_cells = cells // 2
    rows = half_cells // NZ
    orient = directions.shape[1]
    inner = range(1, planes - 1)
    last = planes - 1
    count = rows // chunk
    order = list(range(1, count - 1)) + [0, count - 1]
    me = lax.axis_index("space")
    team = lax.rem(me, 2)
    partner = me + 1 - 2 * team
    after = lax.rem(me + 2, devices)
    before = lax.rem(me + devices - 2, devices)

    barrier = pltpu.get_barrier_semaphore()

    @pl.loop(1, devices)
    def _(d):
        pl.semaphore_signal(
            barrier, inc=1, device_id={"space": lax.rem(me + d, devices)}, device_id_type=MESH
        )

    def remote(source, target, send, recv, device):
        return pltpu.make_async_remote_copy(
            src_ref=source, dst_ref=target, send_sem=send, recv_sem=recv,
            device_id={"space": device}, device_id_type=MESH,
        )

    def wide(factor):
        return jnp.concatenate([factor] * (orient // 128), axis=-1)

    def my_half(ref):
        return jnp.where(team == 0, ref[:, :half_cells], ref[:, half_cells:])

    def upright(row):
        return jnp.broadcast_to(row, (128, half_cells)).T.reshape(rows, NZ, 128)

    sign = (1 - 2 * team).astype(F32)
    speed = sign * directions[...]
    pos = courant * jnp.maximum(speed, 0.0)
    neg = courant * jnp.maximum(-speed, 0.0)
    stay = 1.0 - jnp.sum(pos + neg, axis=0, keepdims=True)
    for c in range(3):
        coef[0, c:c + 1] = pos[c:c + 1]
        coef[0, 3 + c:4 + c] = neg[c:c + 1]
        coef[1, c:c + 1] = neg[c:c + 1]
        coef[1, 3 + c:4 + c] = pos[c:c + 1]
    coef[0, 6:7] = stay
    coef[1, 6:7] = stay

    own_at = pl.multiple_of(team * half_cells, half_cells)
    other_at = pl.multiple_of((1 - team) * half_cells, half_cells)
    plane_at = me // 2 * planes + lax.broadcasted_iota(jnp.int32, (planes, 1), 0)
    ramp = slope * plane_at.astype(F32) / (planes * (devices // 2))
    w_own = my_half(fields) + ramp
    w_away = jnp.where(team == 0, fields[:, half_cells:], fields[:, :half_cells]) + ramp
    factor_own = jnp.exp(-0.5 * w_own)
    factor_away = jnp.exp(-0.5 * w_away)
    def prepare(i):
        away = ends[i, pl.ds(other_at, half_cells)].astype(F32).reshape(rows, NZ, orient)
        half_out[i] = (wide(upright(factor_away[i:i + 1])) * away).astype(BF16)
        column[0, i] = upright(factor_own[i:i + 1])
        own = ends[i, pl.ds(own_at, half_cells)].astype(F32).reshape(rows, NZ, orient)
        state[0, 0, i] = (wide(column[0, i]) * own).astype(BF16)

    for i in (last, 0):
        prepare(i)

    pl.semaphore_wait(barrier, devices - 1)

    field_copy = remote(fields, field_in, field_sem.at[0], field_sem.at[1], partner)

    def ends_copy(i, k=0, low=0, size=rows):
        at = pl.ds(low, size)
        return remote(
            half_out.at[i, at], state.at[1, 0, i, at],
            ends_sem.at[0, i, k], ends_sem.at[1, i, k], partner,
        )

    for k in order:
        ends_copy(last, k, k * chunk, chunk).start()
        ends_copy(0, k, k * chunk, chunk).start()
    field_copy.start()
    def x_copy(s, side, k):
        at = pl.ds(k * chunk, chunk)
        return remote(
            x_out.at[s, side, at], x_in.at[s, side, at],
            x_send.at[s, side, k], x_recv.at[s, side, k],
            after if side == 0 else before,
        )

    spans = ((1, planes - 2), (0, 1), (last, 1))

    def y_copy(s, side, span):
        at = pl.ds(*spans[span])
        return remote(
            y_out.at[s, side, at], y_in.at[s, side, at],
            y_send.at[s, side, span], y_recv.at[s, side, span], partner,
        )

    def packed(first, second, c):
        forward = coef[0, c:c + 1].reshape(1, 1, orient) > 0.0
        return jnp.where(forward, first.astype(F32), second.astype(F32)).astype(BF16)

    def send_y(s, span):
        low, size = spans[span]
        at = slice(low, low + size)
        y_out[s, 0, at] = packed(state[0, s, at, rows - 1], state[1, s, at, rows - 1], 1)
        y_copy(s, 0, span).start()
        y_out[s, 1, at] = packed(state[1, s, at, 0], state[0, s, at, 0], 1)
        y_copy(s, 1, span).start()

    def wait_y(s, span):
        y_copy(s, 0, span).wait()
        y_copy(s, 1, span).wait()

    def drift(s, sp, i, y, size):
        def weight(k):
            return coef[sp, k:k + 1].astype(BF16).reshape(1, 1, orient)

        def part(ref, low, high):
            return ref[low:high]

        here = state.at[sp, s, i]
        center = part(here, y, y + size)
        x_before = x_in.at[s, 0] if i == 0 else state.at[sp, s, i - 1]
        x_after = x_in.at[s, 1] if i == last else state.at[sp, s, i + 1]
        if y == 0:
            y_before = jnp.concatenate(
                [y_in[s, 0, i][None], part(here, 0, size - 1)], axis=0
            )
        else:
            y_before = part(here, y - 1, y + size - 1)
        if y + size == rows:
            y_after = jnp.concatenate(
                [part(here, y + 1, rows), y_in[s, 1, i][None]], axis=0
            )
        else:
            y_after = part(here, y + 1, y + size + 1)
        total = weight(6) * center
        total = total + weight(0) * part(x_before, y, y + size)
        total = total + weight(3) * part(x_after, y, y + size)
        total = total + weight(1) * y_before
        total = total + weight(4) * y_after
        total = total + weight(2) * pltpu.roll(center, 1, 1)
        total = total + weight(5) * pltpu.roll(center, NZ - 1, 1)
        return total.astype(BF16)

    def mix(block):
        shape = block.shape
        flat = block.reshape(shape[0] * NZ, orient)
        return jnp.dot(flat, mixing[...], preferred_element_type=F32).reshape(shape)

    def growth(s, sp, i, low, high):
        now = sp if s < HALF else 1 - sp
        then = sp if s + 1 < HALF else 1 - sp
        return wide(column[now, i, low:high] * column[then, i, low:high])

    def advance(s, sp, i):
        for y in range(0, rows, YB):
            moved[y:y + YB] = drift(s, sp, i, y, YB)
        state[sp, s + 1, i] = (growth(s, sp, i, 0, rows) * mix(moved[...])).astype(BF16)

    corners = ((0, last), (1, last), (0, 0), (1, 0))

    def boundary(s, k):
        y = k * chunk
        for n, (sp, i) in enumerate(corners):
            edges[n * chunk:(n + 1) * chunk] = drift(s, sp, i, y, chunk)
        mixed = mix(edges[...])
        grown = []
        for n, (sp, i) in enumerate(corners):
            value = growth(s, sp, i, y, y + chunk) * mixed[n * chunk:(n + 1) * chunk]
            state[sp, s + 1, i, y:y + chunk] = value.astype(BF16)
            grown.append(value)
        if s + 1 < STEPS:
            x_out[s + 1, 0, y:y + chunk] = packed(grown[0], grown[1], 0)
            x_copy(s + 1, 0, k).start()
            x_out[s + 1, 1, y:y + chunk] = packed(grown[3], grown[2], 0)
            x_copy(s + 1, 1, k).start()

    def pair(k, sp, s, sq, t, i):
        product = state[sp, s, i] * state[sq, t, i]
        reduced[k, i] = lane_sum(product.reshape(half_cells, orient))

    def term(k):
        return jnp.concatenate([reduced[k, i] for i in range(planes)], axis=0)

    for k in order:
        for i, side, first in ((last, 0, 0), (0, 1, 1)):
            ends_copy(i, k, k * chunk, chunk).wait()
            at = slice(k * chunk, (k + 1) * chunk)
            x_out[0, side, at] = packed(state[first, 0, i, at], state[1 - first, 0, i, at], 0)
            x_copy(0, side, k).start()
    send_y(0, 1)
    send_y(0, 2)
    for i in inner:
        prepare(i)
        ends_copy(i).start()

    scaled = synthesis[...].astype(F32) * decay[...].reshape(1, orient)
    high = scaled.astype(BF16)
    low = (scaled - high.astype(F32)).astype(BF16)
    matrix = jnp.dot(high, analysis[...], preferred_element_type=F32)
    matrix = matrix + jnp.dot(low, analysis[...], preferred_element_type=F32)
    mixing[...] = (matrix.T + 1.0 / orient).astype(BF16)

    for i in inner:
        ends_copy(i).wait()
    send_y(0, 0)
    field_copy.wait()
    w_other = my_half(field_in) + ramp
    factor_other = jnp.exp(-0.5 * w_other)
    for i in range(planes):
        column[1, i] = upright(factor_other[i:i + 1])

    def part_copy(d):
        return remote(
            part_out, part_in.at[d], part_send.at[d], part_recv.at[d], lax.rem(me + d, devices)
        )

    def middle():
        return jnp.exp(0.5 * (w_own + w_other)) * term(0)

    def send_part():
        local = jnp.sum(middle(), axis=0, keepdims=True)
        local = sum(local[:, k:k + 128] for k in range(0, half_cells, 128))
        part_out[...] = local
        part_in[0] = local

        @pl.loop(1, devices)
        def _(d):
            part_copy(d).start()

    for s in range(STEPS):
        wait_y(s, 0)
        inside = [functools.partial(advance, s, sp, i) for i in inner for sp in (0, 1)]
        if s + 1 < STEPS:
            inside.append(functools.partial(send_y, s + 1, 0))
        work = list(inside)
        if s == HALF:
            early = [functools.partial(pair, 0, 0, HALF, 1, HALF, i) for i in range(planes)]
            work = early + [send_part] + inside
        if s == STEPS - 1:
            for i in range(planes):
                work.append(functools.partial(pair, 1, 0, 1, 1, 3, i))
                work.append(functools.partial(pair, 2, 1, 1, 0, 3, i))
            for i in inner:
                work.append(functools.partial(pair, 3, 0, 0, 1, 4, i))
                work.append(functools.partial(pair, 4, 1, 0, 0, 4, i))
        for n, k in enumerate(order):
            if k == 0:
                wait_y(s, 1)
                wait_y(s, 2)
            x_copy(s, 0, k).wait()
            x_copy(s, 1, k).wait()
            boundary(s, k)
            for task in work[n * len(work) // count:(n + 1) * len(work) // count]:
                task()
        if s + 1 < STEPS:
            send_y(s + 1, 1)
            send_y(s + 1, 2)

    for i in (0, last):
        pair(3, 0, 0, 1, 4, i)
        pair(4, 1, 0, 0, 4, i)

    @pl.loop(1, devices)
    def _(d):
        part_copy(d).wait()

    whole = jnp.sum(jnp.sum(part_in[...], axis=0), axis=1, keepdims=True)
    inverse = (planes * cells * (devices // 2)) / whole

    rho_other = jnp.exp(w_other) * (0.5 * term(4) + term(2)) + 0.5 * middle()
    rho_out[...] = rho_other * inverse
    rho_copy = remote(rho_out, rho_in, rho_sem.at[0], rho_sem.at[1], partner)
    rho_copy.start()
    rho_own = jnp.exp(w_own) * (0.5 * term(3) + term(1)) + 0.5 * middle()
    kept = rho_own * inverse
    rho_copy.wait()
    got = rho_in[...]
    out[:, :half_cells] = jnp.where(team == 0, kept, got)
    out[:, half_cells:] = jnp.where(team == 0, got, kept)


def shards(fields, end_weights, directions, analysis, synthesis, decay_rates):
    devices = lax.axis_size("space")
    planes, cells = fields.shape
    orient = end_weights.shape[0]
    half_cells = cells // 2
    rows = half_cells // NZ
    chunk = rows // 4
    ends = jnp.transpose(end_weights, (1, 2, 0))
    dma = pltpu.SemaphoreType.DMA
    vmem = pl.BlockSpec(memory_space=pltpu.VMEM)
    return pl.pallas_call(
        functools.partial(kernel, devices, chunk),
        out_shape=jax.ShapeDtypeStruct((planes, cells), F32),
        in_specs=[vmem] * 6,
        out_specs=vmem,
        scratch_shapes=[
            pltpu.VMEM((2, STEPS + 1, planes, rows, NZ, orient), BF16),
            pltpu.VMEM((rows, NZ, orient), BF16),
            pltpu.VMEM((4 * chunk, NZ, orient), BF16),
            pltpu.VMEM((orient, orient), BF16),
            pltpu.VMEM((2, planes, rows, NZ, 128), F32),
            pltpu.VMEM((2, 8, orient), F32),
            pltpu.VMEM((planes, cells), F32),
            pltpu.VMEM((planes, rows, NZ, orient), BF16),
            pltpu.VMEM((STEPS, 2, rows, NZ, orient), BF16),
            pltpu.VMEM((STEPS, 2, rows, NZ, orient), BF16),
            pltpu.VMEM((STEPS, 2, planes, NZ, orient), BF16),
            pltpu.VMEM((STEPS, 2, planes, NZ, orient), BF16),
            pltpu.VMEM((5, planes, 1, half_cells), F32),
            pltpu.VMEM((1, 128), F32),
            pltpu.VMEM((devices, 1, 128), F32),
            pltpu.VMEM((planes, half_cells), F32),
            pltpu.VMEM((planes, half_cells), F32),
            dma((2,)),
            dma((2, planes, rows // chunk)),
            dma((STEPS, 2, rows // chunk)),
            dma((STEPS, 2, rows // chunk)),
            dma((STEPS, 2, 3)),
            dma((STEPS, 2, 3)),
            dma((devices,)),
            dma((devices,)),
            dma((2,)),
        ],
        compiler_params=pltpu.CompilerParams(
            collective_id=0, has_side_effects=True, vmem_limit_bytes=32 * 1024 * 1024
        ),
        name="propagate",
    )(fields, ends, directions, analysis, synthesis, decay_rates)


def solution(mesh):
    return jax.shard_map(
        shards,
        mesh=mesh,
        in_specs=(P(("runs", "space"), None), P(None, ("runs", "space"), None), P(), P(), P(), P()),
        out_specs=P(("runs", "space"), None),
        check_vma=False,
    )
```

```python
import functools

import jax
import jax.numpy as jnp
from jax import lax
from jax.experimental import pallas as pl
from jax.experimental.pallas import tpu as pltpu
from jax.sharding import PartitionSpec as P

NZ = 16
STEPS = 4
HALF = STEPS // 2
YB = 4

courant = 0.3
slope = 0.6

MESH = pl.DeviceIdType.MESH
F32 = jnp.float32
BF16 = jnp.bfloat16


def lane_sum(product):
    ones = jnp.ones((8, product.shape[1]), BF16)
    total = lax.dot_general(ones, product, (((1,), (1,)), ((), ())), preferred_element_type=F32)
    return total[0:1]


def kernel(
    devices, chunk, fields, ends, directions, analysis, synthesis, decay, out,
    state, moved, edges, mixing, column, coef, field_in, half_out,
    x_out, x_in, y_out, y_in, reduced, part_out, part_in, rho_out, rho_in,
    field_sem, ends_sem, x_send, x_recv, y_send, y_recv, part_send, part_recv, rho_sem,
):
    planes, cells = fields.shape
    half_cells = cells // 2
    rows = half_cells // NZ
    orient = directions.shape[1]
    inner = range(1, planes - 1)
    last = planes - 1
    count = rows // chunk
    order = list(range(1, count - 1)) + [0, count - 1]
    me = lax.axis_index("space")
    team = lax.rem(me, 2)
    partner = me + 1 - 2 * team
    after = lax.rem(me + 2, devices)
    before = lax.rem(me + devices - 2, devices)

    barrier = pltpu.get_barrier_semaphore()

    @pl.loop(1, devices)
    def _(d):
        pl.semaphore_signal(
            barrier, inc=1, device_id={"space": lax.rem(me + d, devices)}, device_id_type=MESH
        )

    def remote(source, target, send, recv, device):
        return pltpu.make_async_remote_copy(
            src_ref=source, dst_ref=target, send_sem=send, recv_sem=recv,
            device_id={"space": device}, device_id_type=MESH,
        )

    def wide(factor):
        return jnp.concatenate([factor] * (orient // 128), axis=-1)

    def my_half(ref):
        return jnp.where(team == 0, ref[:, :half_cells], ref[:, half_cells:])

    def upright(row):
        return jnp.broadcast_to(row, (128, half_cells)).T.reshape(rows, NZ, 128)

    sign = (1 - 2 * team).astype(F32)
    speed = sign * directions[...]
    pos = courant * jnp.maximum(speed, 0.0)
    neg = courant * jnp.maximum(-speed, 0.0)
    stay = 1.0 - jnp.sum(pos + neg, axis=0, keepdims=True)
    for c in range(3):
        coef[0, c:c + 1] = pos[c:c + 1]
        coef[0, 3 + c:4 + c] = neg[c:c + 1]
        coef[1, c:c + 1] = neg[c:c + 1]
        coef[1, 3 + c:4 + c] = pos[c:c + 1]
    coef[0, 6:7] = stay
    coef[1, 6:7] = stay

    own_at = pl.multiple_of(team * half_cells, half_cells)
    other_at = pl.multiple_of((1 - team) * half_cells, half_cells)
    plane_at = me // 2 * planes + lax.broadcasted_iota(jnp.int32, (planes, 1), 0)
    ramp = slope * plane_at.astype(F32) / (planes * (devices // 2))
    w_own = my_half(fields) + ramp
    w_away = jnp.where(team == 0, fields[:, half_cells:], fields[:, :half_cells]) + ramp
    factor_own = jnp.exp(-0.5 * w_own)
    factor_away = jnp.exp(-0.5 * w_away)

    def prepare_away(i):
        away = ends[i, pl.ds(other_at, half_cells)].astype(F32).reshape(rows, NZ, orient)
        half_out[i] = (wide(upright(factor_away[i:i + 1])) * away).astype(BF16)

    def prepare_own(i):
        column[0, i] = upright(factor_own[i:i + 1])
        own = ends[i, pl.ds(own_at, half_cells)].astype(F32).reshape(rows, NZ, orient)
        state[0, 0, i] = (wide(column[0, i]) * own).astype(BF16)

    for i in (last, 0):
        prepare_away(i)

    pl.semaphore_wait(barrier, devices - 1)

    field_copy = remote(fields, field_in, field_sem.at[0], field_sem.at[1], partner)

    def ends_copy(i, k=0, low=0, size=rows):
        at = pl.ds(low, size)
        return remote(
            half_out.at[i, at], state.at[1, 0, i, at],
            ends_sem.at[0, i, k], ends_sem.at[1, i, k], partner,
        )

    for k in order:
        ends_copy(last, k, k * chunk, chunk).start()
        ends_copy(0, k, k * chunk, chunk).start()
    field_copy.start()
    for i in (last, 0):
        prepare_own(i)

    def x_copy(s, side, k):
        at = pl.ds(k * chunk, chunk)
        return remote(
            x_out.at[s, side, at], x_in.at[s, side, at],
            x_send.at[s, side, k], x_recv.at[s, side, k],
            after if side == 0 else before,
        )

    spans = ((1, planes - 2), (0, 1), (last, 1))

    def y_copy(s, side, span):
        at = pl.ds(*spans[span])
        return remote(
            y_out.at[s, side, at], y_in.at[s, side, at],
            y_send.at[s, side, span], y_recv.at[s, side, span], partner,
        )

    def packed(first, second, c):
        forward = coef[0, c:c + 1].reshape(1, 1, orient) > 0.0
        return jnp.where(forward, first.astype(F32), second.astype(F32)).astype(BF16)

    def send_y(s, span):
        low, size = spans[span]
        at = slice(low, low + size)
        y_out[s, 0, at] = packed(state[0, s, at, rows - 1], state[1, s, at, rows - 1], 1)
        y_copy(s, 0, span).start()
        y_out[s, 1, at] = packed(state[1, s, at, 0], state[0, s, at, 0], 1)
        y_copy(s, 1, span).start()

    def wait_y(s, span):
        y_copy(s, 0, span).wait()
        y_copy(s, 1, span).wait()

    def drift(s, sp, i, y, size):
        def weight(k):
            return coef[sp, k:k + 1].astype(BF16).reshape(1, 1, orient)

        def part(ref, low, high):
            return ref[low:high]

        here = state.at[sp, s, i]
        center = part(here, y, y + size)
        x_before = x_in.at[s, 0] if i == 0 else state.at[sp, s, i - 1]
        x_after = x_in.at[s, 1] if i == last else state.at[sp, s, i + 1]
        if y == 0:
            y_before = jnp.concatenate(
                [y_in[s, 0, i][None], part(here, 0, size - 1)], axis=0
            )
        else:
            y_before = part(here, y - 1, y + size - 1)
        if y + size == rows:
            y_after = jnp.concatenate(
                [part(here, y + 1, rows), y_in[s, 1, i][None]], axis=0
            )
        else:
            y_after = part(here, y + 1, y + size + 1)
        total = weight(6) * center
        total = total + weight(0) * part(x_before, y, y + size)
        total = total + weight(3) * part(x_after, y, y + size)
        total = total + weight(1) * y_before
        total = total + weight(4) * y_after
        total = total + weight(2) * pltpu.roll(center, 1, 1)
        total = total + weight(5) * pltpu.roll(center, NZ - 1, 1)
        return total.astype(BF16)

    def mix(block):
        shape = block.shape
        flat = block.reshape(shape[0] * NZ, orient)
        return jnp.dot(flat, mixing[...], preferred_element_type=F32).reshape(shape)

    def growth(s, sp, i, low, high):
        now = sp if s < HALF else 1 - sp
        then = sp if s + 1 < HALF else 1 - sp
        return wide(column[now, i, low:high] * column[then, i, low:high])

    def advance(s, sp, i):
        for y in range(0, rows, YB):
            moved[y:y + YB] = drift(s, sp, i, y, YB)
        state[sp, s + 1, i] = (growth(s, sp, i, 0, rows) * mix(moved[...])).astype(BF16)

    corners = ((0, last), (1, last), (0, 0), (1, 0))

    def boundary(s, k):
        y = k * chunk
        for n, (sp, i) in enumerate(corners):
            edges[n * chunk:(n + 1) * chunk] = drift(s, sp, i, y, chunk)
        mixed = mix(edges[...])
        grown = []
        for n, (sp, i) in enumerate(corners):
            value = growth(s, sp, i, y, y + chunk) * mixed[n * chunk:(n + 1) * chunk]
            state[sp, s + 1, i, y:y + chunk] = value.astype(BF16)
            grown.append(value)
        if s + 1 < STEPS:
            x_out[s + 1, 0, y:y + chunk] = packed(grown[0], grown[1], 0)
            x_copy(s + 1, 0, k).start()
            x_out[s + 1, 1, y:y + chunk] = packed(grown[3], grown[2], 0)
            x_copy(s + 1, 1, k).start()

    def pair(k, sp, s, sq, t, i):
        product = state[sp, s, i] * state[sq, t, i]
        reduced[k, i] = lane_sum(product.reshape(half_cells, orient))

    def term(k):
        return jnp.concatenate([reduced[k, i] for i in range(planes)], axis=0)

    for k in order:
        for i, side, first in ((last, 0, 0), (0, 1, 1)):
            ends_copy(i, k, k * chunk, chunk).wait()
            at = slice(k * chunk, (k + 1) * chunk)
            x_out[0, side, at] = packed(state[first, 0, i, at], state[1 - first, 0, i, at], 0)
            x_copy(0, side, k).start()
    send_y(0, 1)
    send_y(0, 2)
    for i in inner:
        prepare_away(i)
        ends_copy(i).start()
        prepare_own(i)

    scaled = synthesis[...].astype(F32) * decay[...].reshape(1, orient)
    high = scaled.astype(BF16)
    low = (scaled - high.astype(F32)).astype(BF16)
    matrix = jnp.dot(high, analysis[...], preferred_element_type=F32)
    matrix = matrix + jnp.dot(low, analysis[...], preferred_element_type=F32)
    mixing[...] = (matrix.T + 1.0 / orient).astype(BF16)

    for i in inner:
        ends_copy(i).wait()
    send_y(0, 0)
    field_copy.wait()
    w_other = my_half(field_in) + ramp
    factor_other = jnp.exp(-0.5 * w_other)
    for i in range(planes):
        column[1, i] = upright(factor_other[i:i + 1])

    def part_copy(d):
        return remote(
            part_out, part_in.at[d], part_send.at[d], part_recv.at[d], lax.rem(me + d, devices)
        )

    def middle():
        return jnp.exp(0.5 * (w_own + w_other)) * term(0)

    def send_part():
        local = jnp.sum(middle(), axis=0, keepdims=True)
        local = sum(local[:, k:k + 128] for k in range(0, half_cells, 128))
        part_out[...] = local
        part_in[0] = local

        @pl.loop(1, devices)
        def _(d):
            part_copy(d).start()

    for s in range(STEPS):
        wait_y(s, 0)
        inside = [functools.partial(advance, s, sp, i) for i in inner for sp in (0, 1)]
        if s + 1 < STEPS:
            inside.append(functools.partial(send_y, s + 1, 0))
        work = list(inside)
        if s == HALF:
            early = [functools.partial(pair, 0, 0, HALF, 1, HALF, i) for i in range(planes)]
            work = early + [send_part] + inside
        if s == STEPS - 1:
            for i in range(planes):
                work.append(functools.partial(pair, 1, 0, 1, 1, 3, i))
                work.append(functools.partial(pair, 2, 1, 1, 0, 3, i))
            for i in inner:
                work.append(functools.partial(pair, 3, 0, 0, 1, 4, i))
                work.append(functools.partial(pair, 4, 1, 0, 0, 4, i))
        for n, k in enumerate(order):
            if k == 0:
                wait_y(s, 1)
                wait_y(s, 2)
            x_copy(s, 0, k).wait()
            x_copy(s, 1, k).wait()
            boundary(s, k)
            for task in work[n * len(work) // count:(n + 1) * len(work) // count]:
                task()
        if s + 1 < STEPS:
            send_y(s + 1, 1)
            send_y(s + 1, 2)

    for i in (0, last):
        pair(3, 0, 0, 1, 4, i)
        pair(4, 1, 0, 0, 4, i)

    @pl.loop(1, devices)
    def _(d):
        part_copy(d).wait()

    whole = jnp.sum(jnp.sum(part_in[...], axis=0), axis=1, keepdims=True)
    inverse = (planes * cells * (devices // 2)) / whole

    rho_other = jnp.exp(w_other) * (0.5 * term(4) + term(2)) + 0.5 * middle()
    rho_out[...] = rho_other * inverse
    rho_copy = remote(rho_out, rho_in, rho_sem.at[0], rho_sem.at[1], partner)
    rho_copy.start()
    rho_own = jnp.exp(w_own) * (0.5 * term(3) + term(1)) + 0.5 * middle()
    kept = rho_own * inverse
    rho_copy.wait()
    got = rho_in[...]
    out[:, :half_cells] = jnp.where(team == 0, kept, got)
    out[:, half_cells:] = jnp.where(team == 0, got, kept)


def shards(fields, end_weights, directions, analysis, synthesis, decay_rates):
    devices = lax.axis_size("space")
    planes, cells = fields.shape
    orient = end_weights.shape[0]
    half_cells = cells // 2
    rows = half_cells // NZ
    chunk = rows // 4
    ends = jnp.transpose(end_weights, (1, 2, 0))
    dma = pltpu.SemaphoreType.DMA
    vmem = pl.BlockSpec(memory_space=pltpu.VMEM)
    return pl.pallas_call(
        functools.partial(kernel, devices, chunk),
        out_shape=jax.ShapeDtypeStruct((planes, cells), F32),
        in_specs=[vmem] * 6,
        out_specs=vmem,
        scratch_shapes=[
            pltpu.VMEM((2, STEPS + 1, planes, rows, NZ, orient), BF16),
            pltpu.VMEM((rows, NZ, orient), BF16),
            pltpu.VMEM((4 * chunk, NZ, orient), BF16),
            pltpu.VMEM((orient, orient), BF16),
            pltpu.VMEM((2, planes, rows, NZ, 128), F32),
            pltpu.VMEM((2, 8, orient), F32),
            pltpu.VMEM((planes, cells), F32),
            pltpu.VMEM((planes, rows, NZ, orient), BF16),
            pltpu.VMEM((STEPS, 2, rows, NZ, orient), BF16),
            pltpu.VMEM((STEPS, 2, rows, NZ, orient), BF16),
            pltpu.VMEM((STEPS, 2, planes, NZ, orient), BF16),
            pltpu.VMEM((STEPS, 2, planes, NZ, orient), BF16),
            pltpu.VMEM((5, planes, 1, half_cells), F32),
            pltpu.VMEM((1, 128), F32),
            pltpu.VMEM((devices, 1, 128), F32),
            pltpu.VMEM((planes, half_cells), F32),
            pltpu.VMEM((planes, half_cells), F32),
            dma((2,)),
            dma((2, planes, rows // chunk)),
            dma((STEPS, 2, rows // chunk)),
            dma((STEPS, 2, rows // chunk)),
            dma((STEPS, 2, 3)),
            dma((STEPS, 2, 3)),
            dma((devices,)),
            dma((devices,)),
            dma((2,)),
        ],
        compiler_params=pltpu.CompilerParams(
            collective_id=0, has_side_effects=True, vmem_limit_bytes=32 * 1024 * 1024
        ),
        name="propagate",
    )(fields, ends, directions, analysis, synthesis, decay_rates)


def solution(mesh):
    return jax.shard_map(
        shards,
        mesh=mesh,
        in_specs=(P(("runs", "space"), None), P(None, ("runs", "space"), None), P(), P(), P(), P()),
        out_specs=P(("runs", "space"), None),
        check_vma=False,
    )
```

```python
import functools

import jax
import jax.numpy as jnp
from jax import lax
from jax.experimental import pallas as pl
from jax.experimental.pallas import tpu as pltpu
from jax.sharding import PartitionSpec as P

NZ = 16
STEPS = 4
HALF = STEPS // 2
YB = 4

courant = 0.3
slope = 0.6

MESH = pl.DeviceIdType.MESH
F32 = jnp.float32
BF16 = jnp.bfloat16


def lane_sum(product):
    ones = jnp.ones((8, product.shape[1]), BF16)
    total = lax.dot_general(ones, product, (((1,), (1,)), ((), ())), preferred_element_type=F32)
    return total[0:1]


def kernel(
    devices, chunk, fields, ends, directions, analysis, synthesis, decay, out,
    state, moved, edges, mixing, column, coef, field_in, half_out,
    x_out, x_in, y_out, y_in, reduced, part_out, part_in, rho_out, rho_in,
    field_sem, ends_sem, x_send, x_recv, y_send, y_recv, part_send, part_recv, rho_sem,
):
    planes, cells = fields.shape
    half_cells = cells // 2
    rows = half_cells // NZ
    orient = directions.shape[1]
    inner = range(1, planes - 1)
    last = planes - 1
    count = rows // chunk
    order = list(range(1, count - 1)) + [0, count - 1]
    me = lax.axis_index("space")
    team = lax.rem(me, 2)
    partner = me + 1 - 2 * team
    after = lax.rem(me + 2, devices)
    before = lax.rem(me + devices - 2, devices)

    barrier = pltpu.get_barrier_semaphore()

    @pl.loop(1, devices)
    def _(d):
        pl.semaphore_signal(
            barrier, inc=1, device_id={"space": lax.rem(me + d, devices)}, device_id_type=MESH
        )

    def remote(source, target, send, recv, device):
        return pltpu.make_async_remote_copy(
            src_ref=source, dst_ref=target, send_sem=send, recv_sem=recv,
            device_id={"space": device}, device_id_type=MESH,
        )

    def wide(factor):
        return jnp.concatenate([factor] * (orient // 128), axis=-1)

    def my_half(ref):
        return jnp.where(team == 0, ref[:, :half_cells], ref[:, half_cells:])

    def upright(row):
        return jnp.broadcast_to(row, (128, half_cells)).T.reshape(rows, NZ, 128)

    sign = (1 - 2 * team).astype(F32)
    speed = sign * directions[...]
    pos = courant * jnp.maximum(speed, 0.0)
    neg = courant * jnp.maximum(-speed, 0.0)
    stay = 1.0 - jnp.sum(pos + neg, axis=0, keepdims=True)
    for c in range(3):
        coef[0, c:c + 1] = pos[c:c + 1]
        coef[0, 3 + c:4 + c] = neg[c:c + 1]
        coef[1, c:c + 1] = neg[c:c + 1]
        coef[1, 3 + c:4 + c] = pos[c:c + 1]
    coef[0, 6:7] = stay
    coef[1, 6:7] = stay

    own_at = pl.multiple_of(team * half_cells, half_cells)
    other_at = pl.multiple_of((1 - team) * half_cells, half_cells)
    plane_at = me // 2 * planes + lax.broadcasted_iota(jnp.int32, (planes, 1), 0)
    ramp = slope * plane_at.astype(F32) / (planes * (devices // 2))
    w_own = my_half(fields) + ramp
    w_away = jnp.where(team == 0, fields[:, half_cells:], fields[:, :half_cells]) + ramp
    factor_own = jnp.exp(-0.5 * w_own)
    factor_away = jnp.exp(-0.5 * w_away)

    def prepare_away(i):
        away = ends[i, pl.ds(other_at, half_cells)].astype(F32).reshape(rows, NZ, orient)
        half_out[i] = (wide(upright(factor_away[i:i + 1])) * away).astype(BF16)

    def prepare_own(i):
        column[0, i] = upright(factor_own[i:i + 1])
        own = ends[i, pl.ds(own_at, half_cells)].astype(F32).reshape(rows, NZ, orient)
        state[0, 0, i] = (wide(column[0, i]) * own).astype(BF16)

    for i in (last, 0):
        prepare_away(i)

    pl.semaphore_wait(barrier, devices - 1)

    field_copy = remote(fields, field_in, field_sem.at[0], field_sem.at[1], partner)

    def ends_copy(i, k=0, low=0, size=rows):
        at = pl.ds(low, size)
        return remote(
            half_out.at[i, at], state.at[1, 0, i, at],
            ends_sem.at[0, i, k], ends_sem.at[1, i, k], partner,
        )

    for k in order:
        ends_copy(last, k, k * chunk, chunk).start()
        ends_copy(0, k, k * chunk, chunk).start()
    field_copy.start()
    for i in (last, 0):
        prepare_own(i)

    def x_copy(s, side, k):
        at = pl.ds(k * chunk, chunk)
        return remote(
            x_out.at[s, side, at], x_in.at[s, side, at],
            x_send.at[s, side, k], x_recv.at[s, side, k],
            after if side == 0 else before,
        )

    spans = ((1, planes - 2), (0, 1), (last, 1))

    def y_copy(s, side, span):
        at = pl.ds(*spans[span])
        return remote(
            y_out.at[s, side, at], y_in.at[s, side, at],
            y_send.at[s, side, span], y_recv.at[s, side, span], partner,
        )

    def packed(first, second, c):
        forward = coef[0, c:c + 1].reshape(1, 1, orient) > 0.0
        return jnp.where(forward, first.astype(F32), second.astype(F32)).astype(BF16)

    def send_y(s, span):
        low, size = spans[span]
        at = slice(low, low + size)
        y_out[s, 0, at] = packed(state[0, s, at, rows - 1], state[1, s, at, rows - 1], 1)
        y_copy(s, 0, span).start()
        y_out[s, 1, at] = packed(state[1, s, at, 0], state[0, s, at, 0], 1)
        y_copy(s, 1, span).start()

    def wait_y(s, span):
        y_copy(s, 0, span).wait()
        y_copy(s, 1, span).wait()

    def drift(s, sp, i, y, size):
        def weight(k):
            return coef[sp, k:k + 1].astype(BF16).reshape(1, 1, orient)

        def part(ref, low, high):
            return ref[low:high]

        here = state.at[sp, s, i]
        center = part(here, y, y + size)
        x_before = x_in.at[s, 0] if i == 0 else state.at[sp, s, i - 1]
        x_after = x_in.at[s, 1] if i == last else state.at[sp, s, i + 1]
        if y == 0:
            y_before = jnp.concatenate(
                [y_in[s, 0, i][None], part(here, 0, size - 1)], axis=0
            )
        else:
            y_before = part(here, y - 1, y + size - 1)
        if y + size == rows:
            y_after = jnp.concatenate(
                [part(here, y + 1, rows), y_in[s, 1, i][None]], axis=0
            )
        else:
            y_after = part(here, y + 1, y + size + 1)
        total = weight(6) * center
        total = total + weight(0) * part(x_before, y, y + size)
        total = total + weight(3) * part(x_after, y, y + size)
        total = total + weight(1) * y_before
        total = total + weight(4) * y_after
        total = total + weight(2) * pltpu.roll(center, 1, 1)
        total = total + weight(5) * pltpu.roll(center, NZ - 1, 1)
        return total.astype(BF16)

    def mix(block):
        shape = block.shape
        flat = block.reshape(shape[0] * NZ, orient)
        return jnp.dot(flat, mixing[...], preferred_element_type=F32).reshape(shape)

    def growth(s, sp, i, low, high):
        now = sp if s < HALF else 1 - sp
        then = sp if s + 1 < HALF else 1 - sp
        return wide(column[now, i, low:high] * column[then, i, low:high])

    def advance(s, sp, i):
        for y in range(0, rows, YB):
            moved[y:y + YB] = drift(s, sp, i, y, YB)
        state[sp, s + 1, i] = (growth(s, sp, i, 0, rows) * mix(moved[...])).astype(BF16)

    corners = ((0, last), (1, last), (0, 0), (1, 0))

    def boundary(s, k):
        y = k * chunk
        for n, (sp, i) in enumerate(corners):
            edges[n * chunk:(n + 1) * chunk] = drift(s, sp, i, y, chunk)
        mixed = mix(edges[...])
        grown = []
        for n, (sp, i) in enumerate(corners):
            value = growth(s, sp, i, y, y + chunk) * mixed[n * chunk:(n + 1) * chunk]
            state[sp, s + 1, i, y:y + chunk] = value.astype(BF16)
            grown.append(value)
        if s + 1 < STEPS:
            x_out[s + 1, 0, y:y + chunk] = packed(grown[0], grown[1], 0)
            x_copy(s + 1, 0, k).start()
            x_out[s + 1, 1, y:y + chunk] = packed(grown[3], grown[2], 0)
            x_copy(s + 1, 1, k).start()

    def pair(k, sp, s, sq, t, i):
        product = state[sp, s, i] * state[sq, t, i]
        reduced[k, i] = lane_sum(product.reshape(half_cells, orient))

    def term(k):
        return jnp.concatenate([reduced[k, i] for i in range(planes)], axis=0)

    for k in order:
        for i, side, first in ((last, 0, 0), (0, 1, 1)):
            ends_copy(i, k, k * chunk, chunk).wait()
            at = slice(k * chunk, (k + 1) * chunk)
            x_out[0, side, at] = packed(state[first, 0, i, at], state[1 - first, 0, i, at], 0)
            x_copy(0, side, k).start()
    send_y(0, 1)
    send_y(0, 2)
    for i in inner:
        prepare_away(i)
        ends_copy(i).start()
        prepare_own(i)

    scaled = synthesis[...].astype(F32) * decay[...].reshape(1, orient)
    high = scaled.astype(BF16)
    low = (scaled - high.astype(F32)).astype(BF16)
    matrix = jnp.dot(high, analysis[...], preferred_element_type=F32)
    matrix = matrix + jnp.dot(low, analysis[...], preferred_element_type=F32)
    mixing[...] = (matrix.T + 1.0 / orient).astype(BF16)

    for i in inner:
        ends_copy(i).wait()
    send_y(0, 0)
    field_copy.wait()
    w_other = my_half(field_in) + ramp
    factor_other = jnp.exp(-0.5 * w_other)
    for i in range(planes):
        column[1, i] = upright(factor_other[i:i + 1])

    def part_copy(d):
        return remote(
            part_out, part_in.at[d], part_send.at[d], part_recv.at[d], lax.rem(me + d, devices)
        )

    def middle():
        return jnp.exp(0.5 * (w_own + w_other)) * term(0)

    def send_part():
        local = jnp.sum(middle(), axis=0, keepdims=True)
        local = sum(local[:, k:k + 128] for k in range(0, half_cells, 128))
        part_out[...] = local
        part_in[0] = local

        @pl.loop(1, devices)
        def _(d):
            part_copy(d).start()

    for s in range(STEPS):
        wait_y(s, 0)
        inside = [functools.partial(advance, s, sp, i) for i in inner for sp in (0, 1)]
        if s + 1 < STEPS:
            inside.append(functools.partial(send_y, s + 1, 0))
        work = list(inside)
        if s == HALF:
            early = [functools.partial(pair, 0, 0, HALF, 1, HALF, i) for i in range(planes)]
            work = early + [send_part] + inside
        if s == STEPS - 1:
            for i in range(planes):
                work.append(functools.partial(pair, 1, 0, 1, 1, 3, i))
                work.append(functools.partial(pair, 2, 1, 1, 0, 3, i))
            for i in inner:
                work.append(functools.partial(pair, 3, 0, 0, 1, 4, i))
                work.append(functools.partial(pair, 4, 1, 0, 0, 4, i))
        for n, k in enumerate(order):
            part_of = work[n * len(work) // count:(n + 1) * len(work) // count]
            if s == STEPS - 1:
                for task in part_of:
                    task()
            if k == 0:
                wait_y(s, 1)
                wait_y(s, 2)
            x_copy(s, 0, k).wait()
            x_copy(s, 1, k).wait()
            boundary(s, k)
            if s + 1 < STEPS:
                for task in part_of:
                    task()
        if s + 1 < STEPS:
            send_y(s + 1, 1)
            send_y(s + 1, 2)

    for i in (0, last):
        pair(3, 0, 0, 1, 4, i)
        pair(4, 1, 0, 0, 4, i)

    @pl.loop(1, devices)
    def _(d):
        part_copy(d).wait()

    whole = jnp.sum(jnp.sum(part_in[...], axis=0), axis=1, keepdims=True)
    inverse = (planes * cells * (devices // 2)) / whole

    rho_other = jnp.exp(w_other) * (0.5 * term(4) + term(2)) + 0.5 * middle()
    rho_out[...] = rho_other * inverse
    rho_copy = remote(rho_out, rho_in, rho_sem.at[0], rho_sem.at[1], partner)
    rho_copy.start()
    rho_own = jnp.exp(w_own) * (0.5 * term(3) + term(1)) + 0.5 * middle()
    kept = rho_own * inverse
    rho_copy.wait()
    got = rho_in[...]
    out[:, :half_cells] = jnp.where(team == 0, kept, got)
    out[:, half_cells:] = jnp.where(team == 0, got, kept)


def shards(fields, end_weights, directions, analysis, synthesis, decay_rates):
    devices = lax.axis_size("space")
    planes, cells = fields.shape
    orient = end_weights.shape[0]
    half_cells = cells // 2
    rows = half_cells // NZ
    chunk = rows // 4
    ends = jnp.transpose(end_weights, (1, 2, 0))
    dma = pltpu.SemaphoreType.DMA
    vmem = pl.BlockSpec(memory_space=pltpu.VMEM)
    return pl.pallas_call(
        functools.partial(kernel, devices, chunk),
        out_shape=jax.ShapeDtypeStruct((planes, cells), F32),
        in_specs=[vmem] * 6,
        out_specs=vmem,
        scratch_shapes=[
            pltpu.VMEM((2, STEPS + 1, planes, rows, NZ, orient), BF16),
            pltpu.VMEM((rows, NZ, orient), BF16),
            pltpu.VMEM((4 * chunk, NZ, orient), BF16),
            pltpu.VMEM((orient, orient), BF16),
            pltpu.VMEM((2, planes, rows, NZ, 128), F32),
            pltpu.VMEM((2, 8, orient), F32),
            pltpu.VMEM((planes, cells), F32),
            pltpu.VMEM((planes, rows, NZ, orient), BF16),
            pltpu.VMEM((STEPS, 2, rows, NZ, orient), BF16),
            pltpu.VMEM((STEPS, 2, rows, NZ, orient), BF16),
            pltpu.VMEM((STEPS, 2, planes, NZ, orient), BF16),
            pltpu.VMEM((STEPS, 2, planes, NZ, orient), BF16),
            pltpu.VMEM((5, planes, 1, half_cells), F32),
            pltpu.VMEM((1, 128), F32),
            pltpu.VMEM((devices, 1, 128), F32),
            pltpu.VMEM((planes, half_cells), F32),
            pltpu.VMEM((planes, half_cells), F32),
            dma((2,)),
            dma((2, planes, rows // chunk)),
            dma((STEPS, 2, rows // chunk)),
            dma((STEPS, 2, rows // chunk)),
            dma((STEPS, 2, 3)),
            dma((STEPS, 2, 3)),
            dma((devices,)),
            dma((devices,)),
            dma((2,)),
        ],
        compiler_params=pltpu.CompilerParams(
            collective_id=0, has_side_effects=True, vmem_limit_bytes=32 * 1024 * 1024
        ),
        name="propagate",
    )(fields, ends, directions, analysis, synthesis, decay_rates)


def solution(mesh):
    return jax.shard_map(
        shards,
        mesh=mesh,
        in_specs=(P(("runs", "space"), None), P(None, ("runs", "space"), None), P(), P(), P(), P()),
        out_specs=P(("runs", "space"), None),
        check_vma=False,
    )
```
